32 devices in a mesh: krow: 16 (over z, y, x), col: 2 (over core).
Axes of the slice: x: 2, y: 2, z: 4, core: 2. Of those that a mesh axis runs over, the one named last changes fastest.
Arguments:
- features: bfloat16 [8192, 6144], P('krow', 'col'), may hold values from -9 to 9
- slab: bfloat16 [8192, 512], P('krow', 'col'), may hold values from -9 to 9
- pack_order: int32 [16, 512], P('krow'), may hold values from 0 to 511, each once within a row
- place_order: int32 [16, 512], P('krow'), may hold values from 0 to 511, each once within a row
- start: int32 [1], replicated, may hold values from 128 to 512
Outputs:
- factored: float32 [8192, 1024], P(('krow', 'col'))
The draws below stay inside these ranges and needn't reach their ends.
Inputs may be any that keep to these rules, and one draw needn't show every extreme that they name: Row k of krow device s's sending order is its local row pack_order[s, k]. `place_order`: each krow device's elimination rows are a rearrangement of the rows it receives. Slab columns from start[0] on are not yet computed and are ignored.
All inputs are finite; a program needn't handle non-finite values.
Results may differ from the reference program's by a relative error of at most 0.0003.
Values may be sent and summed in bfloat16 or wider, within the bound.
A program may use at most 64 MiB of HBM per device.

```python
import jax
import jax.numpy as jnp
from jax import lax

F = 6144
PW = 512
R_DEV = 512
ROWS = 8192
PRIOR = 512
N_KROW = 16


def draw_features(key, part):
    first = jax.random.fold_in(key, 11)
    second = jax.random.fold_in(key, 12)
    third = jax.random.fold_in(key, 13)
    latent = jax.random.normal(first, (ROWS, 8), jnp.float32) * 8.0 ** (-0.5)
    basis = jax.random.normal(second, (8, F), jnp.float32)
    noise = 0.5 * jax.random.normal(third, (ROWS, F), jnp.float32)
    values = jnp.dot(latent, basis, precision=lax.Precision.HIGHEST) + noise
    return jnp.clip(values, -9.0, 9.0).astype(jnp.bfloat16)


def draw_slab(key, part):
    first = jax.random.fold_in(key, 21)
    base = jnp.clip(jax.random.normal(first, (ROWS, PRIOR), jnp.float32), -6.0, 6.0)
    rowscale = jnp.ones((ROWS, 1), jnp.float32)
    upper = (jnp.arange(ROWS) < 2 * PW)[:, None]
    scale = jnp.where(upper, 0.002, 1.5 * rowscale)
    return jnp.clip(base * scale, -9.0, 9.0).astype(jnp.bfloat16)


def setup_inputs(seed: int = 0) -> dict:
    streams_of = jax.random.split(jax.random.key(seed), 6)
    features = draw_features(jax.random.fold_in(streams_of[5], 71), 0)
    slab = draw_slab(jax.random.fold_in(streams_of[5], 71), 0)
    pack_order = jax.vmap(lambda own: jax.random.permutation(own, R_DEV))(jax.random.split(streams_of[2], N_KROW)).reshape((N_KROW, R_DEV)).astype(jnp.int32)
    place_order = jax.vmap(lambda own: jax.random.permutation(own, R_DEV))(jax.random.split(streams_of[3], N_KROW)).reshape((N_KROW, R_DEV)).astype(jnp.int32)
    start = jax.random.randint(streams_of[4], (1,), PRIOR // 4, PRIOR + 1).astype(jnp.int32)
    return dict(features=features, slab=slab, pack_order=pack_order, place_order=place_order, start=start)


RIDGE = 0.5

def reference(features, slab, pack_order, place_order, start):
    group = R_DEV // N_KROW
    senders = (jnp.arange(N_KROW)[:, None] * R_DEV + pack_order).reshape(-1).astype(jnp.int32)
    packed = jnp.take(features, senders, axis=0)
    blocks = packed.reshape(N_KROW, N_KROW, group, F)
    arrived = jnp.transpose(blocks, (1, 0, 2, 3)).reshape(ROWS, F)
    placing = (jnp.arange(N_KROW)[:, None] * R_DEV + place_order).reshape(-1).astype(jnp.int32)
    ordered = jnp.take(arrived, placing, axis=0)
    norms = jnp.sum(jnp.square(ordered.astype(jnp.float32)), axis=1)
    kept = (jnp.arange(PRIOR) < start[0])[None, :]
    keep = jnp.where(kept, slab, jnp.zeros((), jnp.bfloat16))
    positions = jnp.arange(ROWS)
    outputs = []
    earlier = None
    for panel in range(2):
        lower = panel * PW
        targets = lower + jnp.arange(PW)
        gram = jnp.dot(ordered.astype(jnp.float32), ordered[lower:lower + PW].T.astype(jnp.float32), preferred_element_type=jnp.float32)
        dist = norms[:, None] + norms[lower:lower + PW][None, :] - 2.0 * gram
        update = jnp.dot(keep.astype(jnp.float32), keep[lower:lower + PW].T.astype(jnp.float32), preferred_element_type=jnp.float32)
        shift = (positions[:, None] == targets[None, :]).astype(jnp.float32)
        matrix = jnp.exp(-dist / (2.0 * F)) + RIDGE * shift - update
        if earlier is not None:
            matrix = matrix - jnp.dot(earlier, earlier[lower:lower + PW].T, precision=lax.Precision.HIGHEST)
        factor = jnp.linalg.cholesky(matrix[lower:lower + PW])
        solved = jax.scipy.linalg.solve_triangular(factor, matrix.T, lower=True).T
        solved = jnp.where((positions >= lower)[:, None], solved, jnp.zeros((), jnp.float32))
        outputs.append(solved)
        earlier = solved
    return jnp.concatenate(outputs, axis=1)
```

```python
import jax
import jax.numpy as jnp
from jax import lax
from jax.experimental import pallas as pl
from jax.experimental.pallas import tpu as pltpu
from jax.sharding import PartitionSpec as P

F = 6144
PW = 512
RIDGE = 0.5
T = 128
HI = lax.Precision.HIGHEST
NT = (((1,), (1,)), ((), ()))


def dot_nt(a, b):
    return lax.dot_general(a, b, NT, precision=HI, preferred_element_type=jnp.float32)


def inverse_factor(block):
    shape = (T, T)
    rows = lax.broadcasted_iota(jnp.int32, shape, 0)
    lanes = lax.broadcasted_iota(jnp.int32, shape, 1)
    a = block
    z = (rows == lanes).astype(jnp.float32)
    done = []
    for low in range(0, T, 8):
        n = T - low
        sub = lax.broadcasted_iota(jnp.int32, (n, T), 0)
        cols = [jnp.broadcast_to(a[:, low + m:low + m + 1], (n, T)) for m in range(8)]
        pivots = jnp.ones((8, T), jnp.float32)
        for j in range(8):
            pivot = cols[j][j:j + 1, :]
            scale = jnp.where(sub > j, cols[j] * (1.0 / pivot), 0.0)
            for m in range(j + 1, 8):
                cols[m] = cols[m] - scale * cols[m][j:j + 1, :]
            if n > 8:
                a = a - scale * a[j:j + 1, :]
            z = z - scale * z[j:j + 1, :]
            pivots = jnp.where(sub[:8] == j, pivot, pivots)
        done.append(z[:8] * lax.rsqrt(pivots))
        a, z = a[8:], z[8:]
    return jnp.concatenate(done, axis=0)


def factor_kernel(top_ref, low_ref, inv_ref):
    size = top_ref.shape[0]
    blocks = size // T
    low_ref[...] = top_ref[...]
    ids = lax.broadcasted_iota(jnp.int32, (size, T), 0)

    def step(k, carry):
        at = pl.ds(pl.multiple_of(k * T, T), T)
        inv = inverse_factor(low_ref[at, at])
        inv_ref[at, :] = inv
        col = dot_nt(low_ref[:, at], inv)
        col = jnp.where(ids >= (k + 1) * T, col, 0.0)
        low_ref[:, at] = col

        def trail(i, c):
            rows = pl.ds(pl.multiple_of(i * T, T), T)
            low_ref[rows, :] = low_ref[rows, :] - dot_nt(low_ref[rows, at], low_ref[:, at])
            return c

        return lax.fori_loop(k + 1, blocks, trail, carry)

    lax.fori_loop(0, blocks, step, 0)


def factor(top):
    size = top.shape[0]
    return pl.pallas_call(
        factor_kernel,
        out_shape=(
            jax.ShapeDtypeStruct((size, size), jnp.float32),
            jax.ShapeDtypeStruct((size, T), jnp.float32),
        ),
        in_specs=[pl.BlockSpec(memory_space=pltpu.VMEM)],
        out_specs=(pl.BlockSpec(memory_space=pltpu.VMEM),) * 2,
        compiler_params=pltpu.CompilerParams(vmem_limit_bytes=40 * 2**20),
        cost_estimate=pl.CostEstimate(flops=2 * 10**10, bytes_accessed=8 * size * size, transcendentals=0),
        name="factor",
    )(top)


def solve_kernel(mat_ref, low_ref, inv_ref, out_ref):
    size = low_ref.shape[0]
    out_ref[...] = mat_ref[...]

    def step(k, carry):
        at = pl.ds(pl.multiple_of(k * T, T), T)
        col = dot_nt(out_ref[:, at], inv_ref[at, :])
        out_ref[...] = out_ref[...] - dot_nt(col, low_ref[:, at])
        out_ref[:, at] = col
        return carry

    lax.fori_loop(0, size // T, step, 0)


def solve(mat, low, inv):
    return pl.pallas_call(
        solve_kernel,
        out_shape=jax.ShapeDtypeStruct(mat.shape, jnp.float32),
        in_specs=[pl.BlockSpec(memory_space=pltpu.VMEM)] * 3,
        out_specs=pl.BlockSpec(memory_space=pltpu.VMEM),
        compiler_params=pltpu.CompilerParams(vmem_limit_bytes=40 * 2**20),
        name="solve",
    )(mat, low, inv)


def rows_of(x, idx):
    return x.at[idx].get(mode="promise_in_bounds")


def shards(features, slab, pack_order, place_order, start):
    rows_dev, feats_dev = features.shape
    prior_dev = slab.shape[1]
    krows = lax.axis_size("krow")
    column_ranks = lax.axis_size("col")
    krow_index = lax.axis_index("krow")
    col_index = lax.axis_index("col")
    group = rows_dev // krows
    top_rows = 2 * PW
    roots = top_rows // rows_dev
    part_rows = rows_dev // column_ranks

    place = place_order[0]
    digits = jnp.stack([place % 128, place // 128], axis=1).astype(jnp.bfloat16)
    digits = jnp.pad(digits, ((0, 0), (0, 126)))
    owned = jnp.concatenate([slab, digits], axis=1)
    pieces = lax.all_to_all(owned, "krow", split_axis=0, concat_axis=0, tiled=True)
    packed = rows_of(features, pack_order[0])
    head = jnp.concatenate([packed[:roots * group], pieces[:roots * group]], axis=1)
    every = lax.all_gather(head, "krow", axis=0, tiled=False)

    extra = every[:, :, feats_dev:].reshape(krows, roots, group, -1)
    extra = jnp.transpose(extra, (1, 0, 2, 3)).reshape(top_rows, -1)
    top_slab = extra[:, :prior_dev]
    top_slab = lax.all_gather(top_slab, "col", axis=1, tiled=True)
    kept = (jnp.arange(top_slab.shape[1]) < start[0])[None, :]
    top_slab = jnp.where(kept, top_slab, jnp.zeros((), jnp.bfloat16))
    places = extra[:, prior_dev:prior_dev + 2].astype(jnp.int32)
    places = places[:, 0] + 128 * places[:, 1]
    owner = jnp.arange(top_rows) // rows_dev
    source = (places // group) * (roots * group) + owner * group + places % group
    top = rows_of(every.reshape(krows * roots * group, -1), source)[:, :feats_dev]
    top_norms = jnp.sum(jnp.square(top.astype(jnp.float32)), axis=1)

    def matrix_of(dist, prior, first):
        update = lax.dot_general(prior, top_slab, NT, preferred_element_type=jnp.float32)
        at = first + jnp.arange(dist.shape[0])
        shift = (at[:, None] == jnp.arange(top_rows)[None, :]).astype(jnp.float32)
        return jnp.exp(-dist / (2.0 * F)) + RIDGE * shift - update

    def dist_of(own, norms):
        gram = lax.dot_general(own, top, NT, preferred_element_type=jnp.float32)
        return norms[:, None] + top_norms[None, :] - 2.0 * gram

    top_dist = lax.psum(dist_of(top, top_norms), "col")
    low, inv = factor(matrix_of(top_dist, top_slab, 0))

    arrived = lax.all_to_all(packed, "krow", split_axis=0, concat_axis=0, tiled=True)
    ordered = rows_of(arrived, place)
    own_norms = jnp.sum(jnp.square(ordered.astype(jnp.float32)), axis=1)
    dist = lax.psum_scatter(dist_of(ordered, own_norms), "col", scatter_dimension=0, tiled=True)
    own_slab = lax.all_to_all(slab, "col", split_axis=0, concat_axis=1, tiled=True)
    first = krow_index * rows_dev + col_index * part_rows
    solved = solve(matrix_of(dist, own_slab, first), low, inv)
    at = first + jnp.arange(part_rows)
    lower = (jnp.arange(top_rows) // PW) * PW
    return jnp.where(at[:, None] >= lower[None, :], solved, 0.0)


def solution(mesh):
    in_specs = (P("krow", "col"), P("krow", "col"), P("krow", None), P("krow", None), P())
    out_specs = P(("krow", "col"), None)
    return jax.shard_map(shards, mesh=mesh, in_specs=in_specs, out_specs=out_specs, check_vma=False)
```

```python
import jax
import jax.numpy as jnp
from jax import lax
from jax.experimental import pallas as pl
from jax.experimental.pallas import tpu as pltpu
from jax.sharding import PartitionSpec as P

F = 6144
PW = 512
RIDGE = 0.5
T = 128
HI = lax.Precision.HIGHEST
NT = (((1,), (1,)), ((), ()))


def dot_nt(a, b):
    return lax.dot_general(a, b, NT, precision=HI, preferred_element_type=jnp.float32)


def inverse_factor(block):
    shape = (T, T)
    rows = lax.broadcasted_iota(jnp.int32, shape, 0)
    lanes = lax.broadcasted_iota(jnp.int32, shape, 1)
    a = block
    z = (rows == lanes).astype(jnp.float32)
    done = []
    for low in range(0, T, 8):
        n = T - low
        sub = lax.broadcasted_iota(jnp.int32, (n, T), 0)
        cols = [jnp.broadcast_to(a[:, low + m:low + m + 1], (n, T)) for m in range(8)]
        pivots = jnp.ones((8, T), jnp.float32)
        for j in range(8):
            pivot = cols[j][j:j + 1, :]
            scale = jnp.where(sub > j, cols[j] * (1.0 / pivot), 0.0)
            for m in range(j + 1, 8):
                cols[m] = cols[m] - scale * cols[m][j:j + 1, :]
            if n > 8:
                a = a - scale * a[j:j + 1, :]
            z = z - scale * z[j:j + 1, :]
            pivots = jnp.where(sub[:8] == j, pivot, pivots)
        done.append(z[:8] * lax.rsqrt(pivots))
        a, z = a[8:], z[8:]
    return jnp.concatenate(done, axis=0)


def factor_kernel(top_ref, low_ref, inv_ref):
    size = top_ref.shape[0]
    blocks = size // T
    low_ref[...] = top_ref[...]
    half = size // 2
    ids = lax.broadcasted_iota(jnp.int32, (half, T), 0)

    def step(k, carry):
        at = pl.ds(pl.multiple_of(k * T, T), T)
        inv_ref[at, :] = inverse_factor(low_ref[at, at])

        def below(h, c):
            rows = pl.ds(pl.multiple_of(h * half, T), half)
            col = dot_nt(low_ref[rows, at], inv_ref[at, :])
            low_ref[rows, at] = jnp.where(ids >= (k + 1) * T - h * half, col, 0.0)
            return c

        lax.fori_loop(0, 2, below, 0)

        def trail(i, c):
            rows = pl.ds(pl.multiple_of(i * T, T), T)
            low_ref[rows, :] = low_ref[rows, :] - dot_nt(low_ref[rows, at], low_ref[:, at])
            return c

        return lax.fori_loop(k + 1, blocks, trail, carry)

    lax.fori_loop(0, blocks, step, 0)


def factor(top):
    size = top.shape[0]
    return pl.pallas_call(
        factor_kernel,
        out_shape=(
            jax.ShapeDtypeStruct((size, size), jnp.float32),
            jax.ShapeDtypeStruct((size, T), jnp.float32),
        ),
        in_specs=[pl.BlockSpec(memory_space=pltpu.VMEM)],
        out_specs=(pl.BlockSpec(memory_space=pltpu.VMEM),) * 2,
        compiler_params=pltpu.CompilerParams(vmem_limit_bytes=40 * 2**20),
        cost_estimate=pl.CostEstimate(flops=2 * 10**10, bytes_accessed=8 * size * size, transcendentals=0),
        name="factor",
    )(top)


def solve_kernel(mat_ref, low_ref, inv_ref, out_ref):
    size = low_ref.shape[0]
    out_ref[...] = mat_ref[...]

    def step(k, carry):
        at = pl.ds(pl.multiple_of(k * T, T), T)
        col = dot_nt(out_ref[:, at], inv_ref[at, :])
        out_ref[...] = out_ref[...] - dot_nt(col, low_ref[:, at])
        out_ref[:, at] = col
        return carry

    lax.fori_loop(0, size // T, step, 0)


def solve(mat, low, inv):
    return pl.pallas_call(
        solve_kernel,
        out_shape=jax.ShapeDtypeStruct(mat.shape, jnp.float32),
        in_specs=[pl.BlockSpec(memory_space=pltpu.VMEM)] * 3,
        out_specs=pl.BlockSpec(memory_space=pltpu.VMEM),
        compiler_params=pltpu.CompilerParams(vmem_limit_bytes=40 * 2**20),
        name="solve",
    )(mat, low, inv)


def rows_of(x, idx):
    return x.at[idx].get(mode="promise_in_bounds")


def over_pair(v, bit):
    pairs = [(i, i ^ bit) for i in range(lax.axis_size("krow"))]
    return jnp.stack([v, lax.ppermute(v, "krow", pairs)])


def over_ring(v, stride):
    total = lax.axis_size("krow")
    length = total // stride
    rows = v.shape[-2]

    def shift(u, by):
        return lax.ppermute(u, "krow", [(i, (i + by * stride) % total) for i in range(total)])

    got = [None] * length
    got[0] = up = down = v
    for hop in range(1, length // 2):
        up, down = shift(up, 1), shift(down, -1)
        got[length - hop], got[hop] = up, down
    first, second = jnp.split(up, 2, axis=-2)[0], jnp.split(down, 2, axis=-2)[1]
    got[length // 2] = jnp.concatenate([shift(first, 1), shift(second, -1)], axis=-2)
    return jnp.stack(got)


def gather_relative(v):
    width = v.shape[1]
    third, sixth = width // 3, width // 6
    a, b = v[:, :third], v[:, third:2 * third]
    c, d = v[:, 2 * third:2 * third + sixth], v[:, 2 * third + sixth:]
    a, b, c, d = over_ring(a, 4), over_ring(b, 4), over_pair(c, 1), over_pair(d, 2)
    a, b, c, d = over_pair(a, 2), over_pair(b, 1), over_pair(c, 2), over_pair(d, 1)
    a, b, c, d = over_pair(a, 1), over_pair(b, 2), over_ring(c, 4), over_ring(d, 4)
    a = jnp.transpose(a, (2, 1, 0, 3, 4))
    b = jnp.transpose(b, (2, 0, 1, 3, 4))
    d = jnp.transpose(d, (0, 2, 1, 3, 4))
    return jnp.concatenate([a, b, c, d], axis=-1)


def col_sum(v):
    ranks = lax.axis_size("col")
    total = v
    for by in range(1, ranks):
        total = total + lax.ppermute(v, "col", [(i, (i + by) % ranks) for i in range(ranks)])
    return total


def shards(features, slab, pack_order, place_order, start):
    rows_dev, feats_dev = features.shape
    prior_dev = slab.shape[1]
    krows = lax.axis_size("krow")
    column_ranks = lax.axis_size("col")
    krow_index = lax.axis_index("krow")
    col_index = lax.axis_index("col")
    group = rows_dev // krows
    top_rows = 2 * PW
    roots = top_rows // rows_dev
    part_rows = rows_dev // column_ranks

    place = place_order[0]
    digits = jnp.stack([place % 128, place // 128], axis=1).astype(jnp.bfloat16)
    digits = jnp.pad(digits, ((0, 0), (0, 126)))
    owned = jnp.concatenate([slab, digits], axis=1)
    pieces = lax.all_to_all(owned, "krow", split_axis=0, concat_axis=0, tiled=True)
    packed = rows_of(features, pack_order[0])
    every = gather_relative(packed[:roots * group])
    extra = lax.all_gather(pieces[:roots * group], "krow", axis=0, tiled=False)
    extra = extra.reshape(krows, roots, group, -1)
    extra = jnp.transpose(extra, (1, 0, 2, 3)).reshape(top_rows, -1)
    top_slab = extra[:, :prior_dev]
    top_slab = lax.all_gather(top_slab, "col", axis=1, tiled=True)
    kept = (jnp.arange(top_slab.shape[1]) < start[0])[None, :]
    top_slab = jnp.where(kept, top_slab, jnp.zeros((), jnp.bfloat16))
    places = extra[:, prior_dev:prior_dev + 2].astype(jnp.int32)
    places = places[:, 0] + 128 * places[:, 1]
    owner = jnp.arange(top_rows) // rows_dev
    sender = places // group
    away = ((sender // 4 - krow_index // 4) % (krows // 4)) * 4 + ((sender % 4) ^ (krow_index % 4))
    source = away * (roots * group) + owner * group + places % group
    top = rows_of(every.reshape(krows * roots * group, -1), source)
    top_norms = jnp.sum(jnp.square(top.astype(jnp.float32)), axis=1)

    def matrix_of(dist, prior, first):
        update = lax.dot_general(prior, top_slab, NT, preferred_element_type=jnp.float32)
        at = first + jnp.arange(dist.shape[0])
        shift = (at[:, None] == jnp.arange(top_rows)[None, :]).astype(jnp.float32)
        return jnp.exp(-dist / (2.0 * F)) + RIDGE * shift - update

    def dist_of(own, norms):
        gram = lax.dot_general(own, top, NT, preferred_element_type=jnp.float32)
        return norms[:, None] + top_norms[None, :] - 2.0 * gram

    top_dist = col_sum(dist_of(top, top_norms))
    low, inv = factor(matrix_of(top_dist, top_slab, 0))

    own_norms = jnp.sum(jnp.square(packed.astype(jnp.float32)), axis=1)
    dist = lax.all_to_all(dist_of(packed, own_norms), "col", split_axis=1, concat_axis=0, tiled=True)
    dist = jnp.sum(dist.reshape(column_ranks, rows_dev, -1), axis=0)
    dist = lax.all_to_all(dist, "krow", split_axis=0, concat_axis=0, tiled=True)
    dist, low, inv = lax.optimization_barrier((dist, low, inv))
    dist = rows_of(dist, place)
    dist = lax.all_to_all(dist, "col", split_axis=0, concat_axis=1, tiled=True)
    own_slab = lax.all_to_all(slab, "col", split_axis=0, concat_axis=1, tiled=True)
    first = krow_index * rows_dev + col_index * part_rows
    solved = solve(matrix_of(dist, own_slab, first), low, inv)
    at = first + jnp.arange(part_rows)
    lower = (jnp.arange(top_rows) // PW) * PW
    return jnp.where(at[:, None] >= lower[None, :], solved, 0.0)


def solution(mesh):
    in_specs = (P("krow", "col"), P("krow", "col"), P("krow", None), P("krow", None), P())
    out_specs = P(("krow", "col"), None)
    return jax.shard_map(shards, mesh=mesh, in_specs=in_specs, out_specs=out_specs, check_vma=False)
```

```python
import jax
import jax.numpy as jnp
from jax import lax
from jax.experimental import pallas as pl
from jax.experimental.pallas import tpu as pltpu
from jax.sharding import PartitionSpec as P

F = 6144
PW = 512
RIDGE = 0.5
T = 128
HI = lax.Precision.HIGHEST
NT = (((1,), (1,)), ((), ()))


def dot_nt(a, b):
    return lax.dot_general(a, b, NT, precision=HI, preferred_element_type=jnp.float32)


def inverse_factor(block):
    shape = (T, T)
    rows = lax.broadcasted_iota(jnp.int32, shape, 0)
    lanes = lax.broadcasted_iota(jnp.int32, shape, 1)
    a = block
    z = (rows == lanes).astype(jnp.float32)
    done = []
    for low in range(0, T, 8):
        n = T - low
        sub = lax.broadcasted_iota(jnp.int32, (n, T), 0)
        cols = [jnp.broadcast_to(a[:, low + m:low + m + 1], (n, T)) for m in range(8)]
        pivots = jnp.ones((8, T), jnp.float32)
        for j in range(8):
            pivot = cols[j][j:j + 1, :]
            scale = jnp.where(sub > j, cols[j] * (1.0 / pivot), 0.0)
            for m in range(j + 1, 8):
                cols[m] = cols[m] - scale * cols[m][j:j + 1, :]
            if n > 8:
                a = a - scale * a[j:j + 1, :]
            z = z - scale * z[j:j + 1, :]
            pivots = jnp.where(sub[:8] == j, pivot, pivots)
        done.append(z[:8] * lax.rsqrt(pivots))
        a, z = a[8:], z[8:]
    return jnp.concatenate(done, axis=0)


def factor_kernel(top_ref, low_ref, inv_ref):
    size = top_ref.shape[0]
    blocks = size // T
    low_ref[...] = top_ref[...]
    half = size // 2
    ids = lax.broadcasted_iota(jnp.int32, (half, T), 0)

    def step(k, carry):
        at = pl.ds(pl.multiple_of(k * T, T), T)
        inv_ref[at, :] = inverse_factor(low_ref[at, at])

        def below(h, c):
            rows = pl.ds(pl.multiple_of(h * half, T), half)
            col = dot_nt(low_ref[rows, at], inv_ref[at, :])
            low_ref[rows, at] = jnp.where(ids >= (k + 1) * T - h * half, col, 0.0)
            return c

        lax.fori_loop(0, 2, below, 0)

        def trail(i, c):
            rows = pl.ds(pl.multiple_of(i * T, T), T)
            low_ref[rows, :] = low_ref[rows, :] - dot_nt(low_ref[rows, at], low_ref[:, at])
            return c

        return lax.fori_loop(k + 1, blocks, trail, carry)

    lax.fori_loop(0, blocks, step, 0)


def factor(top):
    size = top.shape[0]
    return pl.pallas_call(
        factor_kernel,
        out_shape=(
            jax.ShapeDtypeStruct((size, size), jnp.float32),
            jax.ShapeDtypeStruct((size, T), jnp.float32),
        ),
        in_specs=[pl.BlockSpec(memory_space=pltpu.VMEM)],
        out_specs=(pl.BlockSpec(memory_space=pltpu.VMEM),) * 2,
        compiler_params=pltpu.CompilerParams(vmem_limit_bytes=40 * 2**20),
        cost_estimate=pl.CostEstimate(flops=2 * 10**10, bytes_accessed=8 * size * size, transcendentals=0),
        name="factor",
    )(top)


def solve_kernel(mat_ref, low_ref, inv_ref, out_ref):
    size = low_ref.shape[0]
    out_ref[...] = mat_ref[...]

    def step(k, carry):
        at = pl.ds(pl.multiple_of(k * T, T), T)
        col = dot_nt(out_ref[:, at], inv_ref[at, :])
        out_ref[...] = out_ref[...] - dot_nt(col, low_ref[:, at])
        out_ref[:, at] = col
        return carry

    lax.fori_loop(0, size // T, step, 0)


def solve(mat, low, inv):
    return pl.pallas_call(
        solve_kernel,
        out_shape=jax.ShapeDtypeStruct(mat.shape, jnp.float32),
        in_specs=[pl.BlockSpec(memory_space=pltpu.VMEM)] * 3,
        out_specs=pl.BlockSpec(memory_space=pltpu.VMEM),
        compiler_params=pltpu.CompilerParams(vmem_limit_bytes=40 * 2**20),
        name="solve",
    )(mat, low, inv)


def rows_of(x, idx):
    return x.at[idx].get(mode="promise_in_bounds")


def over_pair(v, bit):
    pairs = [(i, i ^ bit) for i in range(lax.axis_size("krow"))]
    return jnp.stack([v, lax.ppermute(v, "krow", pairs)])


def over_ring(v, stride):
    total = lax.axis_size("krow")
    length = total // stride
    rows = v.shape[-2]

    def shift(u, by):
        return lax.ppermute(u, "krow", [(i, (i + by * stride) % total) for i in range(total)])

    got = [None] * length
    got[0] = up = down = v
    for hop in range(1, length // 2):
        up, down = shift(up, 1), shift(down, -1)
        got[length - hop], got[hop] = up, down
    first, second = jnp.split(up, 2, axis=-2)[0], jnp.split(down, 2, axis=-2)[1]
    got[length // 2] = jnp.concatenate([shift(first, 1), shift(second, -1)], axis=-2)
    return jnp.stack(got)


def gather_relative(v):
    width = v.shape[1]
    third, sixth = width // 3, width // 6
    a, b = v[:, :third], v[:, third:2 * third]
    c, d = v[:, 2 * third:2 * third + sixth], v[:, 2 * third + sixth:]
    a, b, c, d = over_ring(a, 4), over_ring(b, 4), over_pair(c, 1), over_pair(d, 2)
    a, b, c, d = over_pair(a, 2), over_pair(b, 1), over_pair(c, 2), over_pair(d, 1)
    a, b, c, d = over_pair(a, 1), over_pair(b, 2), over_ring(c, 4), over_ring(d, 4)
    return a, b, c, d


def col_sum(v):
    ranks = lax.axis_size("col")
    total = v
    for by in range(1, ranks):
        total = total + lax.ppermute(v, "col", [(i, (i + by) % ranks) for i in range(ranks)])
    return total


def shards(features, slab, pack_order, place_order, start):
    rows_dev, feats_dev = features.shape
    prior_dev = slab.shape[1]
    krows = lax.axis_size("krow")
    column_ranks = lax.axis_size("col")
    krow_index = lax.axis_index("krow")
    col_index = lax.axis_index("col")
    group = rows_dev // krows
    top_rows = 2 * PW
    roots = top_rows // rows_dev
    part_rows = rows_dev // column_ranks

    place = place_order[0]
    digits = jnp.stack([place % 128, place // 128], axis=1).astype(jnp.bfloat16)
    digits = jnp.pad(digits, ((0, 0), (0, 126)))
    owned = jnp.concatenate([slab, digits], axis=1)
    owner = jnp.arange(top_rows) // rows_dev
    mine = (owner == krow_index)[:, None]
    extra = jnp.where(mine, jnp.concatenate([owned] * roots, axis=0), jnp.zeros((), jnp.bfloat16))
    extra = lax.psum(extra, "krow")
    packed = rows_of(features, pack_order[0])
    groups = gather_relative(packed[:roots * group])

    top_slab = lax.all_gather(extra[:, :prior_dev], "col", axis=1, tiled=True)
    kept = (jnp.arange(top_slab.shape[1]) < start[0])[None, :]
    top_slab = jnp.where(kept, top_slab, jnp.zeros((), jnp.bfloat16))
    places = extra[:, prior_dev:prior_dev + 2].astype(jnp.int32)
    places = places[:, 0] + 128 * places[:, 1]
    sender = places // group
    ring = krows // 4
    dz = (sender // 4 - krow_index // 4) % ring
    dy = ((sender ^ krow_index) // 2) % 2
    dx = (sender ^ krow_index) % 2
    offsets = ((dx * 2 + dy) * ring + dz, (dy * 2 + dx) * ring + dz, (dz * 2 + dy) * 2 + dx, (dz * 2 + dx) * 2 + dy)
    row = owner * group + places % group
    top = jnp.concatenate(
        [rows_of(v.reshape(-1, v.shape[-1]), away * (roots * group) + row) for v, away in zip(groups, offsets)],
        axis=1,
    )
    top_norms = jnp.sum(jnp.square(top.astype(jnp.float32)), axis=1)

    def matrix_of(dist, prior, first):
        update = lax.dot_general(prior, top_slab, NT, preferred_element_type=jnp.float32)
        at = first + jnp.arange(dist.shape[0])
        shift = (at[:, None] == jnp.arange(top_rows)[None, :]).astype(jnp.float32)
        return jnp.exp(-dist / (2.0 * F)) + RIDGE * shift - update

    def dist_of(own, norms):
        gram = lax.dot_general(own, top, NT, preferred_element_type=jnp.float32)
        return norms[:, None] + top_norms[None, :] - 2.0 * gram

    top_dist = col_sum(dist_of(top, top_norms))
    low, inv = factor(matrix_of(top_dist, top_slab, 0))

    own_norms = jnp.sum(jnp.square(packed.astype(jnp.float32)), axis=1)
    dist = lax.all_to_all(dist_of(packed, own_norms), "col", split_axis=1, concat_axis=0, tiled=True)
    dist = jnp.sum(dist.reshape(column_ranks, rows_dev, -1), axis=0)
    dist = lax.all_to_all(dist, "krow", split_axis=0, concat_axis=0, tiled=True)
    dist, low, inv = lax.optimization_barrier((dist, low, inv))
    dist = rows_of(dist, place)
    dist = lax.all_to_all(dist, "col", split_axis=0, concat_axis=1, tiled=True)
    own_slab = lax.all_to_all(slab, "col", split_axis=0, concat_axis=1, tiled=True)
    first = krow_index * rows_dev + col_index * part_rows
    solved = solve(matrix_of(dist, own_slab, first), low, inv)
    at = first + jnp.arange(part_rows)
    lower = (jnp.arange(top_rows) // PW) * PW
    return jnp.where(at[:, None] >= lower[None, :], solved, 0.0)


def solution(mesh):
    in_specs = (P("krow", "col"), P("krow", "col"), P("krow", None), P("krow", None), P())
    out_specs = P(("krow", "col"), None)
    return jax.shard_map(shards, mesh=mesh, in_specs=in_specs, out_specs=out_specs, check_vma=False)
```

```python
import jax
import jax.numpy as jnp
from jax import lax
from jax.experimental import pallas as pl
from jax.experimental.pallas import tpu as pltpu
from jax.sharding import PartitionSpec as P

F = 6144
PW = 512
RIDGE = 0.5
T = 128
HI = lax.Precision.HIGHEST
NT = (((1,), (1,)), ((), ()))


def dot_nt(a, b):
    return lax.dot_general(a, b, NT, precision=HI, preferred_element_type=jnp.float32)


def inverse_factor(block):
    shape = (T, T)
    rows = lax.broadcasted_iota(jnp.int32, shape, 0)
    lanes = lax.broadcasted_iota(jnp.int32, shape, 1)
    a = block
    z = (rows == lanes).astype(jnp.float32)
    done = []
    for low in range(0, T, 8):
        n = T - low
        sub = lax.broadcasted_iota(jnp.int32, (n, T), 0)
        cols = [jnp.broadcast_to(a[:, low + m:low + m + 1], (n, T)) for m in range(8)]
        pivots = jnp.ones((8, T), jnp.float32)
        for j in range(8):
            pivot = cols[j][j:j + 1, :]
            scale = jnp.where(sub > j, cols[j] * (1.0 / pivot), 0.0)
            for m in range(j + 1, 8):
                cols[m] = cols[m] - scale * cols[m][j:j + 1, :]
            if n > 8:
                a = a - scale * a[j:j + 1, :]
            z = z - scale * z[j:j + 1, :]
            pivots = jnp.where(sub[:8] == j, pivot, pivots)
        done.append(z[:8] * lax.rsqrt(pivots))
        a, z = a[8:], z[8:]
    return jnp.concatenate(done, axis=0)


def factor_kernel(top_ref, low_ref, inv_ref):
    size = top_ref.shape[0]
    blocks = size // T
    low_ref[...] = top_ref[...]
    half = size // 2
    ids = lax.broadcasted_iota(jnp.int32, (half, T), 0)

    def step(k, carry):
        at = pl.ds(pl.multiple_of(k * T, T), T)
        inv_ref[at, :] = inverse_factor(low_ref[at, at])

        def below(h, c):
            rows = pl.ds(pl.multiple_of(h * half, T), half)
            col = dot_nt(low_ref[rows, at], inv_ref[at, :])
            low_ref[rows, at] = jnp.where(ids >= (k + 1) * T - h * half, col, 0.0)
            return c

        lax.fori_loop(0, 2, below, 0)

        def trail(i, c):
            rows = pl.ds(pl.multiple_of(i * T, T), T)
            low_ref[rows, :] = low_ref[rows, :] - dot_nt(low_ref[rows, at], low_ref[:, at])
            return c

        return lax.fori_loop(k + 1, blocks, trail, carry)

    lax.fori_loop(0, blocks, step, 0)


def factor(top):
    size = top.shape[0]
    return pl.pallas_call(
        factor_kernel,
        out_shape=(
            jax.ShapeDtypeStruct((size, size), jnp.float32),
            jax.ShapeDtypeStruct((size, T), jnp.float32),
        ),
        in_specs=[pl.BlockSpec(memory_space=pltpu.VMEM)],
        out_specs=(pl.BlockSpec(memory_space=pltpu.VMEM),) * 2,
        compiler_params=pltpu.CompilerParams(vmem_limit_bytes=40 * 2**20),
        cost_estimate=pl.CostEstimate(flops=2 * 10**10, bytes_accessed=8 * size * size, transcendentals=0),
        name="factor",
    )(top)


def solve_kernel(mat_ref, low_ref, inv_ref, out_ref):
    size = low_ref.shape[0]
    out_ref[...] = mat_ref[...]

    def step(k, carry):
        at = pl.ds(pl.multiple_of(k * T, T), T)
        col = dot_nt(out_ref[:, at], inv_ref[at, :])
        out_ref[...] = out_ref[...] - dot_nt(col, low_ref[:, at])
        out_ref[:, at] = col
        return carry

    lax.fori_loop(0, size // T, step, 0)


def solve(mat, low, inv):
    return pl.pallas_call(
        solve_kernel,
        out_shape=jax.ShapeDtypeStruct(mat.shape, jnp.float32),
        in_specs=[pl.BlockSpec(memory_space=pltpu.VMEM)] * 3,
        out_specs=pl.BlockSpec(memory_space=pltpu.VMEM),
        compiler_params=pltpu.CompilerParams(vmem_limit_bytes=40 * 2**20),
        name="solve",
    )(mat, low, inv)


def rows_of(x, idx):
    return x.at[idx].get(mode="promise_in_bounds")


def over_pair(v, bit):
    pairs = [(i, i ^ bit) for i in range(lax.axis_size("krow"))]
    return jnp.stack([v, lax.ppermute(v, "krow", pairs)])


def over_ring(v, stride):
    total = lax.axis_size("krow")
    length = total // stride
    rows = v.shape[-2]

    def shift(u, by):
        return lax.ppermute(u, "krow", [(i, (i + by * stride) % total) for i in range(total)])

    got = [None] * length
    got[0] = up = down = v
    for hop in range(1, length // 2):
        up, down = shift(up, 1), shift(down, -1)
        got[length - hop], got[hop] = up, down
    first, second = jnp.split(up, 2, axis=-2)[0], jnp.split(down, 2, axis=-2)[1]
    got[length // 2] = jnp.concatenate([shift(first, 1), shift(second, -1)], axis=-2)
    return jnp.stack(got)


def gather_relative(v, more):
    width = v.shape[1]
    third, sixth = width // 3, width // 6
    a, b = v[:, :third], v[:, third:2 * third]
    c, d = v[:, 2 * third:2 * third + sixth], v[:, 2 * third + sixth:]
    c = jnp.concatenate([c, more], axis=1)
    a, b, c, d = over_ring(a, 4), over_ring(b, 4), over_pair(c, 1), over_pair(d, 2)
    a, b, c, d = over_pair(a, 2), over_pair(b, 1), over_pair(c, 2), over_pair(d, 1)
    a, b, c, d = over_pair(a, 1), over_pair(b, 2), over_ring(c, 4), over_ring(d, 4)
    return a, b, c[..., :sixth], d, c[..., sixth:]


def col_sum(v):
    ranks = lax.axis_size("col")
    total = v
    for by in range(1, ranks):
        total = total + lax.ppermute(v, "col", [(i, (i + by) % ranks) for i in range(ranks)])
    return total


def shards(features, slab, pack_order, place_order, start):
    rows_dev, feats_dev = features.shape
    prior_dev = slab.shape[1]
    krows = lax.axis_size("krow")
    column_ranks = lax.axis_size("col")
    krow_index = lax.axis_index("krow")
    col_index = lax.axis_index("col")
    group = rows_dev // krows
    top_rows = 2 * PW
    roots = top_rows // rows_dev
    part_rows = rows_dev // column_ranks

    place = place_order[0]
    digits = jnp.stack([place % 128, place // 128], axis=1).astype(jnp.bfloat16)
    digits = jnp.pad(digits, ((0, 0), (0, 126)))
    owned = jnp.concatenate([slab, digits], axis=1)
    owner = jnp.arange(top_rows) // rows_dev
    pieces = lax.all_to_all(owned, "krow", split_axis=0, concat_axis=0, tiled=True)
    packed = rows_of(features, pack_order[0])
    *groups, extra = gather_relative(packed[:roots * group], pieces[:roots * group])
    ring = krows // 4

    def steps(sender):
        dz = (sender // 4 - krow_index // 4) % ring
        return dz, ((sender ^ krow_index) // 2) % 2, (sender ^ krow_index) % 2

    within = jnp.arange(top_rows) % rows_dev
    dz, dy, dx = steps(within // group)
    source = ((dz * 2 + dy) * 2 + dx) * (roots * group) + owner * group + within % group
    extra = rows_of(extra.reshape(-1, extra.shape[-1]), source)

    top_slab = lax.all_gather(extra[:, :prior_dev], "col", axis=1, tiled=True)
    kept = (jnp.arange(top_slab.shape[1]) < start[0])[None, :]
    top_slab = jnp.where(kept, top_slab, jnp.zeros((), jnp.bfloat16))
    places = extra[:, prior_dev:prior_dev + 2].astype(jnp.int32)
    places = places[:, 0] + 128 * places[:, 1]
    sender = places // group
    dz, dy, dx = steps(sender)
    offsets = ((dx * 2 + dy) * ring + dz, (dy * 2 + dx) * ring + dz, (dz * 2 + dy) * 2 + dx, (dz * 2 + dx) * 2 + dy)
    row = owner * group + places % group
    top = jnp.concatenate(
        [rows_of(v.reshape(-1, v.shape[-1]), away * (roots * group) + row) for v, away in zip(groups, offsets)],
        axis=1,
    )
    top_norms = jnp.sum(jnp.square(top.astype(jnp.float32)), axis=1)

    def matrix_of(dist, prior, first):
        update = lax.dot_general(prior, top_slab, NT, preferred_element_type=jnp.float32)
        at = first + jnp.arange(dist.shape[0])
        shift = (at[:, None] == jnp.arange(top_rows)[None, :]).astype(jnp.float32)
        return jnp.exp(-dist / (2.0 * F)) + RIDGE * shift - update

    def dist_of(own, norms):
        gram = lax.dot_general(own, top, NT, preferred_element_type=jnp.float32)
        return norms[:, None] + top_norms[None, :] - 2.0 * gram

    top_dist = col_sum(dist_of(top, top_norms))
    low, inv = factor(matrix_of(top_dist, top_slab, 0))

    own_norms = jnp.sum(jnp.square(packed.astype(jnp.float32)), axis=1)
    dist = lax.all_to_all(dist_of(packed, own_norms), "col", split_axis=1, concat_axis=0, tiled=True)
    dist = jnp.sum(dist.reshape(column_ranks, rows_dev, -1), axis=0)
    dist = lax.all_to_all(dist, "krow", split_axis=0, concat_axis=0, tiled=True)
    dist, low, inv = lax.optimization_barrier((dist, low, inv))
    dist = rows_of(dist, place)
    dist = lax.all_to_all(dist, "col", split_axis=0, concat_axis=1, tiled=True)
    own_slab = lax.all_to_all(slab, "col", split_axis=0, concat_axis=1, tiled=True)
    first = krow_index * rows_dev + col_index * part_rows
    solved = solve(matrix_of(dist, own_slab, first), low, inv)
    at = first + jnp.arange(part_rows)
    lower = (jnp.arange(top_rows) // PW) * PW
    return jnp.where(at[:, None] >= lower[None, :], solved, 0.0)


def solution(mesh):
    in_specs = (P("krow", "col"), P("krow", "col"), P("krow", None), P("krow", None), P())
    out_specs = P(("krow", "col"), None)
    return jax.shard_map(shards, mesh=mesh, in_specs=in_specs, out_specs=out_specs, check_vma=False)
```
